512 devices in a mesh: gx: 32 (over z, core), gy: 16 (over y, x).
Axes of the slice: x: 4, y: 4, z: 16, core: 2. Of those that a mesh axis runs over, the one named last changes fastest.
Arguments:
- operator: float32 [32, 16, 768, 768], P('gx', 'gy'), may hold values from -2 to 3, as said below
- loads: float32 [32, 16, 256, 768], P('gx', 'gy'), may hold values from -80 to 80
- warm: float32 [32, 16, 256, 768], P('gx', 'gy'), may hold values from -6 to 6
- orders: int32 [32, 16], replicated, may hold values from 256 to 768, as said below
- face_x: int32 [32, 16, 128], P('gx', 'gy'), may hold values from 0 to 767, as said below
- face_y: int32 [32, 16, 128], P('gx', 'gy'), may hold values from 0 to 767, as said below
- contact: int32 [32, 16, 768], P('gx', 'gy'), may hold values 0 or 1
Outputs:
- multipliers: float32 [32, 16, 256, 768], P('gx', 'gy')
The draws below stay inside these ranges and needn't reach their ends.
Inputs may be any that keep to these rules, and one draw needn't show every extreme that they name: `orders`: multiples of 128; every draw has a subdomain of order 768; the orders of subdomains [i, j] and [(i + 16) mod 32, j] add up to 1024. `face_x`: 128 distinct rows of the subdomain, each below its order. `face_y`: 128 distinct rows of the subdomain, each below its order. `operator`: each matrix has a positive diagonal of order one.
All inputs are finite; a program needn't handle non-finite values. No bound on the sum of `contact` on one device may be relied on, other than what follows from the above.
Results may differ from the reference program's by a relative error of at most 0.00018.
Values sent between devices are 32-bit elements; how exact they have to be, the bound alone decides.
No kernel may reach another device: no remote copies, remote signals or barrier semaphores. Data moves between devices by JAX's collectives and lax.ppermute only.
A program may use at most 64 MiB of HBM per device.

```python
import jax
import jax.numpy as jnp
from jax import lax

ORDER = 768
STRIP = 128
STRIPS = 6
FSLOT = 128
COLS = 256
ITERS = 3
SUB_X = 32
SUB_Y = 16


def subdomain_orders(key):
    base = jax.random.fold_in(key, 7)
    keys = jax.random.split(base, 3)
    half_x = SUB_X // 2
    first = jax.random.randint(keys[0], (half_x, SUB_Y), 2, STRIPS + 1)
    where_x = jax.random.randint(keys[1], (), 0, half_x)
    where_y = jax.random.randint(keys[2], (), 0, SUB_Y)
    first = first.at[where_x, where_y].set(STRIPS)
    second = STRIPS + 2 - first
    counts = jnp.concatenate([first, second], axis=0)
    return (counts * STRIP).astype(jnp.int32)


def face_rows(key, salt):
    order_table = subdomain_orders(key)
    salted = jax.random.fold_in(key, salt)
    row_index = jnp.arange(ORDER, dtype=jnp.int32)
    ranking = jax.random.randint(salted, (SUB_X, SUB_Y, ORDER), 0, 2 ** 20) * ORDER + row_index[None, None, :]
    ranking = jnp.where(row_index[None, None, :] < order_table[:, :, None], ranking, ranking + 2 ** 30)
    ordering = jnp.argsort(ranking, axis=-1)
    return ordering[:, :, :FSLOT].astype(jnp.int32)


def draw_orders(key, part):
    return subdomain_orders(key)


def draw_face_x(key, part):
    return face_rows(key, 11)


def draw_face_y(key, part):
    return face_rows(key, 13)


def draw_operator(key, part):
    keys = jax.random.split(jax.random.fold_in(key, 21), 2)
    shape = (SUB_X, SUB_Y, ORDER, ORDER)
    offdiag = jax.random.truncated_normal(keys[0], -4.0, 4.0, shape, jnp.float32) * 0.5 / jnp.sqrt(float(ORDER))
    diagonal = jax.random.uniform(keys[1], (SUB_X, SUB_Y, ORDER), jnp.float32, 0.8, 1.2)
    identity = jnp.eye(ORDER, dtype=jnp.float32)
    return (offdiag + diagonal[:, :, :, None] * identity[None, None, :, :]).astype(jnp.float32)


def draw_loads(key, part):
    keys = jax.random.split(jax.random.fold_in(key, 31), 2)
    shape = (SUB_X, SUB_Y, COLS, ORDER)
    position = (jnp.arange(SUB_X, dtype=jnp.float32)[:, None] / (SUB_X - 1) + jnp.arange(SUB_Y, dtype=jnp.float32)[None, :] / (SUB_Y - 1)) / 2.0
    row_scale = jnp.exp(jax.random.uniform(keys[1], (SUB_X, SUB_Y, 1, ORDER), jnp.float32, jnp.log(0.3), jnp.log(3.0)))
    values = jax.random.truncated_normal(keys[0], -4.0, 4.0, shape, jnp.float32)
    rising = 1.0 + 2.0 * position
    return (0.5 * values * row_scale * rising[:, :, None, None]).astype(jnp.float32)


def set_ends(values, rng, low, high):
    longest = values.shape.index(max(values.shape))
    spots = []
    for shift in (0, 1):
        where = [jax.random.randint(jax.random.fold_in(rng, axis), (), 0, length) for axis, length in enumerate(values.shape)]
        where[longest] = (where[longest] + shift) % values.shape[longest]
        spots.append(tuple(where))
    return values.at[spots[0]].set(low).at[spots[1]].set(high)


def levels(rng, extent, pieces, least, high):
    level = 1.0
    for dim, parts in pieces:
        heights = jax.random.uniform(jax.random.fold_in(jax.random.fold_in(rng, 6), dim), (parts,), jnp.float32, least / len(pieces), high / len(pieces))
        level = level * jnp.repeat(jnp.exp(heights), extent[dim] // parts).reshape((-1,) + (1,) * (len(extent) - 1 - dim))
    return level


def bell_draw(stream_key, extent, scale, limit, shards=(), kind=jnp.bfloat16):
    loudness = levels(stream_key, extent, shards, -0.22, 0.18) if shards else 1.0
    entries = jax.random.normal(stream_key, extent, jnp.float32) * scale * loudness
    return jnp.minimum(jnp.maximum(entries, -limit), limit).astype(kind)


def setup_inputs(seed: int = 0) -> dict:
    key_of = jax.random.split(jax.random.key(seed), 8)
    operator = draw_operator(jax.random.fold_in(key_of[7], 71), 0)
    loads = draw_loads(jax.random.fold_in(key_of[7], 71), 0)
    warm = bell_draw(key_of[2], (SUB_X, SUB_Y, COLS, ORDER), 1.0, 6.0, ((0, 32), (1, 16)), jnp.float32)
    orders = draw_orders(jax.random.fold_in(key_of[7], 71), 0)
    face_x = draw_face_x(jax.random.fold_in(key_of[7], 71), 0)
    face_y = draw_face_y(jax.random.fold_in(key_of[7], 71), 0)
    contact = set_ends((jax.random.randint(key_of[6], (SUB_X, SUB_Y, ORDER), 0, 3) < 1).astype(jnp.int32), jax.random.fold_in(key_of[6], 1), 0, 1)
    return dict(operator=operator, loads=loads, warm=warm, orders=orders, face_x=face_x, face_y=face_y, contact=contact)


step_length = 0.5
epsilon = 1e-06

def place_jumps(products, rows_x, sum_x, rows_y, sum_y):
    return products.at[:, rows_x].add(-sum_x).at[:, rows_y].add(-sum_y)

def reference(operator, loads, warm, orders, face_x, face_y, contact):
    row_index = jnp.arange(ORDER, dtype=jnp.int32)
    live_mask = (row_index[None, None, :] < orders[:, :, None]).astype(jnp.float32)[:, :, None, :]
    multipliers = warm * live_mask
    rhs = loads * live_mask
    index_x = jnp.broadcast_to(face_x[:, :, None, :], (SUB_X, SUB_Y, COLS, FSLOT))
    index_y = jnp.broadcast_to(face_y[:, :, None, :], (SUB_X, SUB_Y, COLS, FSLOT))
    placer = jax.vmap(jax.vmap(place_jumps))
    for iteration in range(ITERS):
        products = jnp.einsum('xyco,xyro->xycr', multipliers, operator, precision=lax.Precision.HIGHEST) * live_mask
        near_x = jnp.take_along_axis(products, index_x, axis=3)
        near_y = jnp.take_along_axis(products, index_y, axis=3)
        padded_x = jnp.pad(near_x, ((1, 1), (0, 0), (0, 0), (0, 0)))
        sum_x = padded_x[:-2] + padded_x[2:]
        padded_y = jnp.pad(near_y, ((0, 0), (1, 1), (0, 0), (0, 0)))
        sum_y = padded_y[:, :-2] + padded_y[:, 2:]
        jumps = placer(products, face_x, sum_x, face_y, sum_y)
        gradient = jumps - rhs
        squares = lax.optimization_barrier(jnp.sum(gradient * gradient, axis=(0, 1, 3)))
        spread = jnp.sqrt(squares / (SUB_X * SUB_Y * ORDER) + epsilon)
        multipliers = multipliers - step_length * gradient / spread[None, None, :, None]
        multipliers = jnp.where(contact[:, :, None, :] == 1, jnp.maximum(multipliers, 0.0), multipliers)
    return multipliers
```

```python
import jax
import jax.numpy as jnp
from jax import lax
from jax.experimental import pallas as pl
from jax.experimental.pallas import tpu as pltpu
from jax.sharding import Mesh
from jax.sharding import PartitionSpec as P

ORDER = 768
FSLOT = 128
COLS = 256
ITERS = 3
GX = ("z", "c")
GY = ("y", "x")
NEAR = ("c", "y", "x")
FAR = ("z",)

step_length = 0.5
epsilon = 1e-06

f32 = jnp.float32
bf16 = jnp.bfloat16


def dot(a, b):
    return lax.dot_general(a, b, (((1,), (0,)), ((), ())), preferred_element_type=f32)


def split(x):
    high = x.astype(bf16)
    return high, (x - high.astype(f32)).astype(bf16)


def product(a_high, a_low, m_high, m_low):
    return dot(a_high, m_high) + (dot(a_high, m_low) + dot(a_low, m_high))


def live_rows(order, columns):
    return lax.broadcasted_iota(jnp.int32, (ORDER, columns), 0) < order


def first_kernel(place, orders, operator, warm, face_x, face_y,
                 high_out, low_out, faces_high_out, faces_low_out, spots_out, m_out, m_high_out, m_low_out, near_x_out, near_y_out):
    order = orders[place[1], place[0]]
    m = jnp.where(live_rows(order, COLS), warm[...].T, 0.0)
    m_out[...] = m
    m_high, m_low = split(m)
    m_high_out[...] = m_high
    m_low_out[...] = m_low
    high, low = split(jnp.where(live_rows(order, ORDER), operator[...], 0.0))
    high_out[...] = high
    low_out[...] = low
    rows = lax.broadcasted_iota(jnp.int32, (ORDER, FSLOT), 0)
    spots_out[:, :FSLOT] = jnp.where(rows == face_x[...], 1.0, 0.0).astype(bf16)
    spots_out[:, FSLOT:] = jnp.where(rows == face_y[...], 1.0, 0.0).astype(bf16)
    for number, (face, near_out) in enumerate(((face_x, near_x_out), (face_y, near_y_out))):
        column = jnp.broadcast_to(face[...].astype(f32), (FSLOT, FSLOT)).T
        wide = jnp.concatenate([column] * (ORDER // FSLOT), axis=1)
        lanes = lax.broadcasted_iota(jnp.int32, (FSLOT, ORDER), 1).astype(f32)
        pick = jnp.where(wide == lanes, 1.0, 0.0).astype(bf16)
        face_high = dot(pick, high).astype(bf16)
        face_low = dot(pick, low).astype(bf16)
        faces_high_out[number * FSLOT : (number + 1) * FSLOT, :] = face_high
        faces_low_out[number * FSLOT : (number + 1) * FSLOT, :] = face_low
        near_out[...] = product(face_high, face_low, m_high, m_low)


def first_main_kernel(place, orders, high, low, m_high, m_low, loads, contact, local_out, rhs_out, floor_out):
    order = orders[place[1], place[0]]
    rhs = jnp.where(live_rows(order, COLS), loads[...].T, 0.0)
    rhs_out[...] = rhs
    floor = jnp.where(contact[...] == 1, 0.0, -jnp.inf)
    floor_out[...] = jnp.broadcast_to(floor, (FSLOT, ORDER)).T
    local_out[...] = product(high[...], low[...], m_high[...], m_low[...]) - rhs


def main_kernel(high, low, m_high, m_low, rhs, local_out):
    local_out[...] = product(high[...], low[...], m_high[...], m_low[...]) - rhs[...]


def gradient_kernel(local, spots, left, right, below, above, gradient_out, squares_out):
    sums = jnp.concatenate([left[...] + right[...], below[...] + above[...]], axis=0)
    sum_high, sum_low = split(sums)
    gradient = local[...] - (dot(spots[...], sum_high) + dot(spots[...], sum_low))
    gradient_out[...] = gradient
    squares_out[...] = jnp.sum(gradient * gradient, axis=0, keepdims=True)


def updated(everything, m, gradient, floor, count):
    squares = jnp.sum(everything[...], axis=0)
    rate = step_length / jnp.sqrt(squares / count + epsilon)
    lowest = jnp.concatenate([floor[...]] * (COLS // FSLOT), axis=1)
    return jnp.maximum(m[...] - gradient[...] * rate, lowest)


def update_kernel(count, everything, m, gradient, floor, faces_high, faces_low, m_out, m_high_out, m_low_out, near_x_out, near_y_out):
    new = updated(everything, m, gradient, floor, count)
    m_out[...] = new
    m_high, m_low = split(new)
    m_high_out[...] = m_high
    m_low_out[...] = m_low
    near = product(faces_high[...], faces_low[...], m_high, m_low)
    near_x_out[...] = near[:FSLOT]
    near_y_out[...] = near[FSLOT:]


def last_kernel(count, everything, m, gradient, floor, out):
    out[...] = updated(everything, m, gradient, floor, count).T


VMEM = pl.BlockSpec(memory_space=pltpu.VMEM)
SMEM = pl.BlockSpec(memory_space=pltpu.SMEM)


def call(kernel, name, out, *args, scalars=0):
    shapes = tuple(pltpu.VMEM(shape, dtype) for shape, dtype in out)
    args = [*args[:scalars], *(pltpu.with_memory_space_constraint(arg, pltpu.VMEM) for arg in args[scalars:])]
    result = pl.pallas_call(
        kernel,
        name=name,
        out_shape=shapes,
        in_specs=[SMEM] * scalars + [VMEM] * (len(args) - scalars),
        out_specs=tuple(VMEM for _ in shapes),
        compiler_params=pltpu.CompilerParams(vmem_limit_bytes=24 * 2**20),
    )(*args)
    return result


def passed_along(block, axis, distance):
    devices = range(lax.axis_size(axis))
    route = [(i - distance, i) for i in devices if i - distance in devices]
    return lax.ppermute(block, axis, route)


def from_everyone(x, axis):
    copies = jnp.broadcast_to(x[None], (lax.axis_size(axis), *x.shape))
    return lax.all_to_all(copies, axis, split_axis=0, concat_axis=0, tiled=True)


def body(operator, loads, warm, orders, face_x, face_y, contact):
    count = float(lax.axis_size(GX) * lax.axis_size(GY) * ORDER)
    place = jnp.stack([lax.axis_index(GX), lax.axis_index(GY)]).astype(jnp.int32)
    square = ((ORDER, ORDER), bf16)
    faces = ((2 * FSLOT, ORDER), bf16)
    state = ((ORDER, COLS), f32)
    half = ((ORDER, COLS), bf16)
    face = ((FSLOT, COLS), f32)
    high, low, faces_high, faces_low, spots, m, m_high, m_low, near_x, near_y = call(
        first_kernel, "first",
        [square, square, faces, faces, ((ORDER, 2 * FSLOT), bf16), state, half, half, face, face],
        place, orders.T, operator[0, 0], warm[0, 0], face_x[0], face_y[0], scalars=2,
    )
    for iteration in range(ITERS):
        below = passed_along(near_y, GY, 1)
        above = passed_along(near_y, GY, -1)
        left = passed_along(near_x, GX, 1)
        right = passed_along(near_x, GX, -1)
        if iteration == 0:
            local, rhs, floor = call(
                first_main_kernel, "first_main", [state, state, ((ORDER, FSLOT), f32)],
                place, orders.T, high, low, m_high, m_low, loads[0, 0], contact[0], scalars=2,
            )
        else:
            (local,) = call(main_kernel, "main", [state], high, low, m_high, m_low, rhs)
        gradient, squares = call(
            gradient_kernel, "gradient", [state, ((1, COLS), f32)], local, spots, left, right, below, above
        )
        squares = jnp.sum(from_everyone(squares, NEAR), axis=0)
        everything = from_everyone(squares, FAR)
        if iteration < ITERS - 1:
            m, m_high, m_low, near_x, near_y = call(
                lambda *refs: update_kernel(count, *refs), "update", [state, half, half, face, face],
                everything, m, gradient, floor, faces_high, faces_low,
            )
        else:
            (out,) = call(lambda *refs: last_kernel(count, *refs), "last", [((COLS, ORDER), f32)], everything, m, gradient, floor)
    return out[None, None]


def solution(mesh):
    shape = dict(mesh.shape)
    finer = Mesh(mesh.devices.reshape(shape["gx"] // 2, 2, 4, shape["gy"] // 4), ("z", "c", "y", "x"))
    in_specs = (
        P(GX, GY, None, None),
        P(GX, GY, None, None),
        P(GX, GY, None, None),
        P(),
        P(GX, GY, None),
        P(GX, GY, None),
        P(GX, GY, None),
    )
    out_specs = P(GX, GY, None, None)
    return jax.shard_map(body, mesh=finer, in_specs=in_specs, out_specs=out_specs, check_vma=False)
```

```python
import functools

import jax
import jax.numpy as jnp
from jax import lax
from jax.experimental import pallas as pl
from jax.experimental.pallas import tpu as pltpu
from jax.sharding import Mesh
from jax.sharding import PartitionSpec as P

ORDER = 768
FSLOT = 128
COLS = 256
ITERS = 3
CHUNKS = ORDER // COLS
GX = ("z", "c")
GY = ("y", "x")
NEAR = ("c", "y", "x")
FAR = ("z",)

step_length = 0.5
epsilon = 1e-06

f32 = jnp.float32
bf16 = jnp.bfloat16


def dot(a, b):
    return lax.dot_general(a, b, (((1,), (0,)), ((), ())), preferred_element_type=f32)


def split(x):
    high = x.astype(bf16)
    return high, (x - high.astype(f32)).astype(bf16)


def product(a_high, a_low, m_high, m_low):
    return dot(a_high, m_high) + (dot(a_high, m_low) + dot(a_low, m_high))


def live_rows(order, columns):
    return lax.broadcasted_iota(jnp.int32, (ORDER, columns), 0) < order


def chunk(number):
    return slice(number * COLS, (number + 1) * COLS)


def chunk_copies(source, target, sems):
    copies = [
        pltpu.make_async_copy(source.at[pl.ds(number * COLS, COLS), :], target.at[pl.ds(number * COLS, COLS), :], sems.at[number])
        for number in range(CHUNKS)
    ]
    for copy in copies:
        copy.start()
    return copies


def first_kernel(place, orders, operator, warm, face_x, face_y, contact,
                 faces_high_out, faces_low_out, slots_out, floor_out, m_out, m_high_out, m_low_out, near_x_out, near_y_out,
                 rows_here, sems):
    copies = chunk_copies(operator, rows_here, sems)
    order = orders[place[1], place[0]]
    m = jnp.where(live_rows(order, COLS), warm[...].T, 0.0)
    m_out[...] = m
    m_high, m_low = split(m)
    m_high_out[...] = m_high
    m_low_out[...] = m_low
    floor = jnp.where(contact[...] == 1, 0.0, -jnp.inf)
    floor_out[...] = jnp.broadcast_to(floor, (FSLOT, ORDER)).T.astype(bf16)
    slots_out[0:1, :] = face_x[...]
    slots_out[1:2, :] = face_y[...]
    column = jnp.concatenate([jnp.broadcast_to(face[...].astype(f32), (FSLOT, FSLOT)).T for face in (face_x, face_y)], axis=0)
    wide = jnp.concatenate([column] * (COLS // FSLOT), axis=1)
    lanes = lax.broadcasted_iota(jnp.int32, (2 * FSLOT, COLS), 1)
    face_high = jnp.zeros((2 * FSLOT, ORDER), f32)
    face_low = jnp.zeros((2 * FSLOT, ORDER), f32)
    for number, copy in enumerate(copies):
        pick = jnp.where(wide == (lanes + number * COLS).astype(f32), 1.0, 0.0).astype(bf16)
        copy.wait()
        high, low = split(rows_here[chunk(number), :])
        face_high += dot(pick, high)
        face_low += dot(pick, low)
    face_high = face_high.astype(bf16)
    face_low = face_low.astype(bf16)
    faces_high_out[...] = face_high
    faces_low_out[...] = face_low
    near = product(face_high, face_low, m_high, m_low)
    near_x_out[...] = near[:FSLOT]
    near_y_out[...] = near[FSLOT:]


def main_kernel(place, orders, operator, loads, m_high, m_low, local_out, rows_here, loads_here, sems, loads_sem):
    copies = chunk_copies(operator, rows_here, sems)
    loads_copy = pltpu.make_async_copy(loads, loads_here, loads_sem)
    loads_copy.start()
    order = orders[place[1], place[0]]
    for number, copy in enumerate(copies):
        copy.wait()
        high, low = split(rows_here[chunk(number), :])
        local_out[chunk(number), :] = product(high, low, m_high[...], m_low[...])
    loads_copy.wait()
    live = live_rows(order, COLS)
    local_out[...] = jnp.where(live, local_out[...] - loads_here[...].T, 0.0)


def gradient_kernel(slots, local, left, right, below, above, gradient_out, squares_out):
    rows = lax.broadcasted_iota(jnp.int32, (ORDER, FSLOT), 0)
    spots = jnp.concatenate([jnp.where(rows == slots[number : number + 1, :], 1.0, 0.0).astype(bf16) for number in range(2)], axis=1)
    sums = jnp.concatenate([left[...] + right[...], below[...] + above[...]], axis=0)
    sum_high, sum_low = split(sums)
    gradient = local[...] - (dot(spots, sum_high) + dot(spots, sum_low))
    gradient_out[...] = gradient
    squares_out[...] = jnp.sum(gradient * gradient, axis=0, keepdims=True)


def updated(everything, m, gradient, floor, count):
    squares = jnp.sum(everything[...], axis=0)
    rate = step_length / jnp.sqrt(squares / count + epsilon)
    lowest = jnp.concatenate([floor[...].astype(f32)] * (COLS // FSLOT), axis=1)
    return jnp.maximum(m[...] - gradient[...] * rate, lowest)


def update_kernel(count, everything, m, gradient, floor, faces_high, faces_low, m_out, m_high_out, m_low_out, near_x_out, near_y_out):
    new = updated(everything, m, gradient, floor, count)
    m_out[...] = new
    m_high, m_low = split(new)
    m_high_out[...] = m_high
    m_low_out[...] = m_low
    near = product(faces_high[...], faces_low[...], m_high, m_low)
    near_x_out[...] = near[:FSLOT]
    near_y_out[...] = near[FSLOT:]


def last_kernel(count, everything, m, gradient, floor, out, out_here, sems):
    squares = jnp.sum(everything[...], axis=0)
    rate = step_length / jnp.sqrt(squares / count + epsilon)
    copies = []
    for number in range(CHUNKS):
        part = chunk(number)
        lowest = jnp.concatenate([floor[part, :].astype(f32)] * (COLS // FSLOT), axis=1)
        out_here[:, part] = jnp.maximum(m[part, :] - gradient[part, :] * rate, lowest).T
        where = pl.ds(number * COLS, COLS)
        copies.append(pltpu.make_async_copy(out_here.at[:, where], out.at[:, where], sems.at[number]))
        copies[-1].start()
    for copy in copies:
        copy.wait()


HERE = pl.BlockSpec(memory_space=pltpu.VMEM)
SMEM = pl.BlockSpec(memory_space=pltpu.SMEM)
ANY = pl.BlockSpec(memory_space=pl.ANY)


def outside(x):
    return pltpu.with_memory_space_constraint(x, pltpu.HBM)


def scalar(x):
    return x, SMEM


def far(x):
    return outside(x), ANY


def loaded(x):
    return outside(x), HERE


def kept(x):
    return pltpu.with_memory_space_constraint(x, pltpu.VMEM), HERE


def keep(shape, dtype):
    return pltpu.VMEM(shape, dtype), HERE


def call(kernel, name, outs, args, scratch=()):
    return pl.pallas_call(
        kernel,
        name=name,
        out_shape=tuple(shape for shape, _ in outs),
        in_specs=[spec for _, spec in args],
        out_specs=tuple(spec for _, spec in outs),
        scratch_shapes=list(scratch),
        compiler_params=pltpu.CompilerParams(vmem_limit_bytes=24 * 2**20),
    )(*(arg for arg, _ in args))


def passed_along(block, axis, distance):
    devices = range(lax.axis_size(axis))
    route = [(i - distance, i) for i in devices if i - distance in devices]
    return lax.ppermute(block, axis, route)


def from_everyone(x, axis):
    copies = jnp.broadcast_to(x[None], (lax.axis_size(axis), *x.shape))
    return lax.all_to_all(copies, axis, split_axis=0, concat_axis=0, tiled=True)


def body(operator, loads, warm, orders, face_x, face_y, contact):
    count = float(lax.axis_size(GX) * lax.axis_size(GY) * ORDER)
    place = jnp.stack([lax.axis_index(GX), lax.axis_index(GY)]).astype(jnp.int32)
    here = [scalar(place), scalar(outside(orders.T))]
    faces = keep((2 * FSLOT, ORDER), bf16)
    state = keep((ORDER, COLS), f32)
    half = keep((ORDER, COLS), bf16)
    face = keep((FSLOT, COLS), f32)
    rows_here = pltpu.VMEM((ORDER, ORDER), f32)
    loads_here = pltpu.VMEM((COLS, ORDER), f32)
    sems = pltpu.SemaphoreType.DMA((CHUNKS,))
    faces_high, faces_low, slots, floor, m, m_high, m_low, near_x, near_y = call(
        first_kernel, "first",
        [faces, faces, keep((2, FSLOT), jnp.int32), keep((ORDER, FSLOT), bf16), state, half, half, face, face],
        [*here, far(operator[0, 0]), loaded(warm[0, 0]), loaded(face_x[0]), loaded(face_y[0]), loaded(contact[0])],
        [rows_here, sems],
    )
    for iteration in range(ITERS):
        below = passed_along(near_y, GY, 1)
        above = passed_along(near_y, GY, -1)
        left = passed_along(near_x, GX, 1)
        right = passed_along(near_x, GX, -1)
        (local,) = call(
            main_kernel, "main", [state],
            [*here, far(operator[0, 0]), far(loads[0, 0]), kept(m_high), kept(m_low)],
            [rows_here, loads_here, sems, pltpu.SemaphoreType.DMA],
        )
        gradient, squares = call(
            gradient_kernel, "gradient", [state, keep((1, COLS), f32)],
            [kept(x) for x in (slots, local, left, right, below, above)],
        )
        squares = jnp.sum(from_everyone(squares, NEAR), axis=0)
        everything = from_everyone(squares, FAR)
        given = [kept(x) for x in (everything, m, gradient, floor)]
        if iteration < ITERS - 1:
            m, m_high, m_low, near_x, near_y = call(
                functools.partial(update_kernel, count), "update", [state, half, half, face, face],
                [*given, kept(faces_high), kept(faces_low)],
            )
        else:
            (out,) = call(
                functools.partial(last_kernel, count), "last",
                [(pltpu.HBM((COLS, ORDER), f32), ANY)], given, [loads_here, sems],
            )
    return out[None, None]


def solution(mesh):
    shape = dict(mesh.shape)
    finer = Mesh(mesh.devices.reshape(shape["gx"] // 2, 2, 4, shape["gy"] // 4), ("z", "c", "y", "x"))
    in_specs = (
        P(GX, GY, None, None),
        P(GX, GY, None, None),
        P(GX, GY, None, None),
        P(),
        P(GX, GY, None),
        P(GX, GY, None),
        P(GX, GY, None),
    )
    out_specs = P(GX, GY, None, None)
    return jax.shard_map(body, mesh=finer, in_specs=in_specs, out_specs=out_specs, check_vma=False)
```

```python
import functools

import jax
import jax.numpy as jnp
from jax import lax
from jax.experimental import pallas as pl
from jax.experimental.pallas import tpu as pltpu
from jax.sharding import Mesh
from jax.sharding import PartitionSpec as P

ORDER = 768
FSLOT = 128
COLS = 256
ITERS = 3
CHUNKS = ORDER // COLS
GX = ("z", "c")
GY = ("y", "x")
NEAR = ("c", "y", "x")
FAR = ("z",)

step_length = 0.5
epsilon = 1e-06

f32 = jnp.float32
bf16 = jnp.bfloat16


def dot(a, b):
    return lax.dot_general(a, b, (((1,), (0,)), ((), ())), preferred_element_type=f32)


def split(x):
    high = x.astype(bf16)
    return high, (x - high.astype(f32)).astype(bf16)


def product(a_high, a_low, m_high, m_low):
    return dot(a_high, m_high) + (dot(a_high, m_low) + dot(a_low, m_high))


def live_rows(order, columns):
    return lax.broadcasted_iota(jnp.int32, (ORDER, columns), 0) < order


def chunk(number):
    return slice(number * COLS, (number + 1) * COLS)


def chunk_copies(source, target, sems):
    copies = [
        pltpu.make_async_copy(source.at[:, pl.ds(number * COLS, COLS)], target.at[:, pl.ds(number * COLS, COLS)], sems.at[number])
        for number in range(CHUNKS)
    ]
    for copy in copies:
        copy.start()
    return copies


def first_kernel(orders, operator, warm, face_x, face_y, contact,
                 high_out, low_out, faces_high_out, faces_low_out, slots_out, floor_out, m_out, m_high_out, m_low_out, near_x_out, near_y_out,
                 orders_here, rows_here, warm_here, contact_here, sems, small_sems):
    small = [
        pltpu.make_async_copy(face_x, slots_out.at[0:1, :], small_sems.at[0]),
        pltpu.make_async_copy(face_y, slots_out.at[1:2, :], small_sems.at[1]),
        pltpu.make_async_copy(orders, orders_here, small_sems.at[2]),
        pltpu.make_async_copy(warm, warm_here, small_sems.at[3]),
        pltpu.make_async_copy(contact, contact_here, small_sems.at[4]),
    ]
    for copy in small:
        copy.start()
    copies = chunk_copies(operator, rows_here, sems)
    small[0].wait()
    small[1].wait()
    column = jnp.concatenate([jnp.broadcast_to(slots_out[n : n + 1, :].astype(f32), (FSLOT, FSLOT)).T for n in range(2)], axis=0)
    wide = jnp.concatenate([column] * (ORDER // FSLOT), axis=1)
    lanes = lax.broadcasted_iota(jnp.int32, (2 * FSLOT, ORDER), 1).astype(f32)
    pick = jnp.where(wide == lanes, 1.0, 0.0).astype(bf16)
    small[4].wait()
    floor = jnp.where(contact_here[...] == 1, 0.0, -jnp.inf)
    floor_out[...] = jnp.broadcast_to(floor, (FSLOT, ORDER)).T.astype(bf16)
    small[2].wait()
    small[3].wait()
    order = order_of(orders_here)
    m = jnp.where(live_rows(order, COLS), warm_here[...].T, 0.0)
    m_out[...] = m
    m_high, m_low = split(m)
    m_high_out[...] = m_high
    m_low_out[...] = m_low
    near = jnp.zeros((2 * FSLOT, COLS), f32)
    for number, copy in enumerate(copies):
        copy.wait()
        part = chunk(number)
        high, low = split(jnp.where(live_rows(order, COLS), rows_here[:, part], 0.0))
        high_out[:, part] = high
        low_out[:, part] = low
        face_high = dot(pick, high).astype(bf16)
        face_low = dot(pick, low).astype(bf16)
        faces_high_out[:, part] = face_high
        faces_low_out[:, part] = face_low
        near += product(face_high, face_low, m_high_out[part, :], m_low_out[part, :])
    near_x_out[...] = near[:FSLOT]
    near_y_out[...] = near[FSLOT:]


def order_of(orders):
    return orders[lax.axis_index(GY), lax.axis_index(GX)]


def first_main_kernel(orders, high, low, m_high, m_low, loads, local_out, rhs_out, orders_here, orders_sem):
    copy = pltpu.make_async_copy(orders, orders_here, orders_sem)
    copy.start()
    total = product(high[...], low[...], m_high[...], m_low[...])
    copy.wait()
    rhs = jnp.where(live_rows(order_of(orders_here), COLS), loads[...].T, 0.0)
    rhs_out[...] = rhs
    local_out[...] = total - rhs


def main_kernel(high, low, m_high, m_low, rhs, local_out):
    local_out[...] = product(high[...], low[...], m_high[...], m_low[...]) - rhs[...]


def middle_kernel(everything, out):
    total = jnp.sum(everything[...], axis=0)
    out[...] = jnp.broadcast_to(total[None], out.shape)


def gradient_kernel(slots, local, outer, inner, below, above, gradient_out, squares_out):
    rows = lax.broadcasted_iota(jnp.int32, (ORDER, FSLOT), 0)
    spots = jnp.concatenate([jnp.where(rows == slots[number : number + 1, :], 1.0, 0.0).astype(bf16) for number in range(2)], axis=1)
    sums = jnp.concatenate([outer[...] + inner[...], below[...] + above[...]], axis=0)
    sum_high, sum_low = split(sums)
    gradient = local[...] - (dot(spots, sum_high) + dot(spots, sum_low))
    gradient_out[...] = gradient
    squares = jnp.sum(gradient * gradient, axis=0, keepdims=True)
    squares_out[...] = jnp.broadcast_to(squares[None], squares_out.shape)


def updated(everything, m, gradient, floor, count):
    squares = jnp.sum(everything[...], axis=0)
    rate = step_length / jnp.sqrt(squares / count + epsilon)
    lowest = jnp.concatenate([floor[...].astype(f32)] * (COLS // FSLOT), axis=1)
    return jnp.maximum(m[...] - gradient[...] * rate, lowest)


def update_kernel(count, everything, m, gradient, floor, faces_high, faces_low, m_out, m_high_out, m_low_out, near_x_out, near_y_out):
    new = updated(everything, m, gradient, floor, count)
    m_out[...] = new
    m_high, m_low = split(new)
    m_high_out[...] = m_high
    m_low_out[...] = m_low
    near = product(faces_high[...], faces_low[...], m_high, m_low)
    near_x_out[...] = near[:FSLOT]
    near_y_out[...] = near[FSLOT:]


def last_kernel(count, everything, m, gradient, floor, out, out_here, sems):
    squares = jnp.sum(everything[...], axis=0)
    rate = step_length / jnp.sqrt(squares / count + epsilon)
    copies = []
    for number in range(CHUNKS):
        part = chunk(number)
        lowest = jnp.concatenate([floor[part, :].astype(f32)] * (COLS // FSLOT), axis=1)
        out_here[:, part] = jnp.maximum(m[part, :] - gradient[part, :] * rate, lowest).T
        where = pl.ds(number * COLS, COLS)
        copies.append(pltpu.make_async_copy(out_here.at[:, where], out.at[:, where], sems.at[number]))
        copies[-1].start()
    for copy in copies:
        copy.wait()


HERE = pl.BlockSpec(memory_space=pltpu.VMEM)
ANY = pl.BlockSpec(memory_space=pl.ANY)


def outside(x):
    return pltpu.with_memory_space_constraint(x, pltpu.HBM)


def far(x):
    return outside(x), ANY


def kept(x):
    return pltpu.with_memory_space_constraint(x, pltpu.VMEM), HERE


def keep(shape, dtype):
    return pltpu.VMEM(shape, dtype), HERE


def call(kernel, outs, args, scratch=()):
    return pl.pallas_call(
        kernel,
        out_shape=tuple(shape for shape, _ in outs),
        in_specs=[spec for _, spec in args],
        out_specs=tuple(spec for _, spec in outs),
        scratch_shapes=list(scratch),
        compiler_params=pltpu.CompilerParams(vmem_limit_bytes=24 * 2**20),
    )(*(arg for arg, _ in args))


def swapped(block, axis, first):
    route = []
    for i in range(first, lax.axis_size(axis) - 1, 2):
        route += [(i, i + 1), (i + 1, i)]
    return lax.ppermute(block, axis, route)


def from_everyone(copies, axis):
    return lax.all_to_all(copies, axis, split_axis=0, concat_axis=0, tiled=True)


def body(operator, loads, warm, orders, face_x, face_y, contact):
    count = float(lax.axis_size(GX) * lax.axis_size(GY) * ORDER)
    orders = orders.T
    square = keep((ORDER, ORDER), bf16)
    faces = keep((2 * FSLOT, ORDER), bf16)
    state = keep((ORDER, COLS), f32)
    half = keep((ORDER, COLS), bf16)
    face = keep((FSLOT, COLS), f32)
    rows_here = pltpu.VMEM((ORDER, ORDER), f32)
    orders_here = pltpu.SMEM(orders.shape, jnp.int32)
    loads_here = pltpu.VMEM((COLS, ORDER), f32)
    sems = pltpu.SemaphoreType.DMA((CHUNKS,))
    high, low, faces_high, faces_low, slots, floor, m, m_high, m_low, near_x, near_y = call(
        first_kernel,
        [square, square, faces, faces, keep((2, FSLOT), jnp.int32), keep((ORDER, FSLOT), bf16), state, half, half, face, face],
        [far(x) for x in (orders, operator[0, 0], warm[0, 0], face_x[0], face_y[0], contact[0])],
        [orders_here, rows_here, loads_here, pltpu.VMEM((1, ORDER), jnp.int32), sems, pltpu.SemaphoreType.DMA((5,))],
    )
    for iteration in range(ITERS):
        below = swapped(near_y, GY, 0)
        above = swapped(near_y, GY, 1)
        outer = swapped(near_x, GX, 1)
        inner = swapped(near_x, GX, 0)
        matrices = [kept(x) for x in (high, low, m_high, m_low)]
        if iteration == 0:
            local, rhs = call(
                first_main_kernel, [state, state], [far(orders), *matrices, kept(loads[0, 0])],
                [orders_here, pltpu.SemaphoreType.DMA],
            )
        else:
            (local,) = call(main_kernel, [state], [*matrices, kept(rhs)])
        gradient, squares = call(
            gradient_kernel, [state, keep((lax.axis_size(NEAR), 1, COLS), f32)],
            [kept(x) for x in (slots, local, outer, inner, below, above)],
        )
        (squares,) = call(
            middle_kernel, [keep((lax.axis_size(FAR), 1, COLS), f32)], [kept(from_everyone(squares, NEAR))]
        )
        everything = from_everyone(squares, FAR)
        given = [kept(x) for x in (everything, m, gradient, floor)]
        if iteration < ITERS - 1:
            m, m_high, m_low, near_x, near_y = call(
                functools.partial(update_kernel, count), [state, half, half, face, face],
                [*given, kept(faces_high), kept(faces_low)],
            )
        else:
            (out,) = call(
                functools.partial(last_kernel, count),
                [(pltpu.HBM((COLS, ORDER), f32), ANY)], given, [loads_here, sems],
            )
    return out[None, None]


def solution(mesh):
    shape = dict(mesh.shape)
    finer = Mesh(mesh.devices.reshape(shape["gx"] // 2, 2, 4, shape["gy"] // 4), ("z", "c", "y", "x"))
    in_specs = (
        P(GX, GY, None, None),
        P(GX, GY, None, None),
        P(GX, GY, None, None),
        P(),
        P(GX, GY, None),
        P(GX, GY, None),
        P(GX, GY, None),
    )
    out_specs = P(GX, GY, None, None)
    return jax.shard_map(body, mesh=finer, in_specs=in_specs, out_specs=out_specs, check_vma=False)
```

```python
import functools

import jax
import jax.numpy as jnp
from jax import lax
from jax.experimental import pallas as pl
from jax.experimental.pallas import tpu as pltpu
from jax.sharding import Mesh
from jax.sharding import PartitionSpec as P

ORDER = 768
FSLOT = 128
COLS = 256
ITERS = 3
CHUNKS = ORDER // COLS
GX = ("z", "c")
GY = ("y", "x")
NEAR = ("c", "y", "x")
FAR = ("z",)

step_length = 0.5
epsilon = 1e-06

f32 = jnp.float32
bf16 = jnp.bfloat16


def dot(a, b):
    return lax.dot_general(a, b, (((1,), (0,)), ((), ())), preferred_element_type=f32)


def split(x):
    high = x.astype(bf16)
    return high, (x - high.astype(f32)).astype(bf16)


def product(a_high, a_low, m_high, m_low):
    return dot(a_high, m_high) + (dot(a_high, m_low) + dot(a_low, m_high))


def live_rows(order, columns):
    return lax.broadcasted_iota(jnp.int32, (ORDER, columns), 0) < order


def chunk(number):
    return slice(number * COLS, (number + 1) * COLS)


def chunk_copies(source, target, sems):
    return [
        pltpu.make_async_copy(source.at[:, pl.ds(number * COLS, COLS)], target.at[:, pl.ds(number * COLS, COLS)], sems.at[number])
        for number in range(CHUNKS)
    ]


def first_kernel(orders, operator, warm, loads, face_x, face_y, contact,
                 high_out, low_out, faces_high_out, faces_low_out, slots_out, floor_out, rhs_out, m_out, m_high_out, m_low_out, near_x_out, near_y_out,
                 orders_here, rows_here, warm_here, loads_here, contact_here, sems, small_sems):
    small = [
        pltpu.make_async_copy(face_x, slots_out.at[0:1, :], small_sems.at[0]),
        pltpu.make_async_copy(face_y, slots_out.at[1:2, :], small_sems.at[1]),
        pltpu.make_async_copy(orders, orders_here, small_sems.at[2]),
        pltpu.make_async_copy(warm, warm_here, small_sems.at[3]),
        pltpu.make_async_copy(contact, contact_here, small_sems.at[4]),
        pltpu.make_async_copy(loads, loads_here, small_sems.at[5]),
    ]
    for copy in small[:5]:
        copy.start()
    copies = chunk_copies(operator, rows_here, sems)
    for copy in copies:
        copy.start()
    small[5].start()
    small[0].wait()
    small[1].wait()
    column = jnp.concatenate([jnp.broadcast_to(slots_out[n : n + 1, :].astype(f32), (FSLOT, FSLOT)).T for n in range(2)], axis=0)
    wide = jnp.concatenate([column] * (ORDER // FSLOT), axis=1)
    lanes = lax.broadcasted_iota(jnp.int32, (2 * FSLOT, ORDER), 1).astype(f32)
    pick = jnp.where(wide == lanes, 1.0, 0.0).astype(bf16)
    small[4].wait()
    floor = jnp.where(contact_here[...] == 1, 0.0, -jnp.inf)
    floor_out[...] = jnp.broadcast_to(floor, (FSLOT, ORDER)).T.astype(bf16)
    small[2].wait()
    small[3].wait()
    order = order_of(orders_here)
    m = jnp.where(live_rows(order, COLS), warm_here[...].T, 0.0)
    m_out[...] = m
    m_high, m_low = split(m)
    m_high_out[...] = m_high
    m_low_out[...] = m_low
    near = jnp.zeros((2 * FSLOT, COLS), f32)
    for number, copy in enumerate(copies):
        copy.wait()
        if number == 1:
            small[5].wait()
            rhs_out[...] = jnp.where(live_rows(order, COLS), loads_here[...].T, 0.0)
        part = chunk(number)
        high, low = split(jnp.where(live_rows(order, COLS), rows_here[:, part], 0.0))
        high_out[:, part] = high
        low_out[:, part] = low
        face_high = dot(pick, high).astype(bf16)
        face_low = dot(pick, low).astype(bf16)
        faces_high_out[:, part] = face_high
        faces_low_out[:, part] = face_low
        near += product(face_high, face_low, m_high_out[part, :], m_low_out[part, :])
    near_x_out[...] = near[:FSLOT]
    near_y_out[...] = near[FSLOT:]


def order_of(orders):
    return orders[lax.axis_index(GY), lax.axis_index(GX)]


def main_kernel(high, low, m_high, m_low, rhs, local_out):
    local_out[...] = product(high[...], low[...], m_high[...], m_low[...]) - rhs[...]


def middle_kernel(everything, out):
    total = jnp.sum(everything[...], axis=0)
    out[...] = jnp.broadcast_to(total[None], out.shape)


def gradient_kernel(slots, local, outer, inner, below, above, gradient_out, squares_out):
    rows = lax.broadcasted_iota(jnp.int32, (ORDER, FSLOT), 0)
    spots = jnp.concatenate([jnp.where(rows == slots[number : number + 1, :], 1.0, 0.0).astype(bf16) for number in range(2)], axis=1)
    sums = jnp.concatenate([outer[...] + inner[...], below[...] + above[...]], axis=0)
    sum_high, sum_low = split(sums)
    gradient = local[...] - (dot(spots, sum_high) + dot(spots, sum_low))
    gradient_out[...] = gradient
    squares = jnp.sum(gradient * gradient, axis=0, keepdims=True)
    squares_out[...] = jnp.broadcast_to(squares[None], squares_out.shape)


def updated(everything, m, gradient, floor, count):
    squares = jnp.sum(everything[...], axis=0)
    rate = step_length / jnp.sqrt(squares / count + epsilon)
    lowest = jnp.concatenate([floor[...].astype(f32)] * (COLS // FSLOT), axis=1)
    return jnp.maximum(m[...] - gradient[...] * rate, lowest)


def update_kernel(count, everything, m, gradient, floor, faces_high, faces_low, m_out, m_high_out, m_low_out, near_x_out, near_y_out):
    new = updated(everything, m, gradient, floor, count)
    m_out[...] = new
    m_high, m_low = split(new)
    m_high_out[...] = m_high
    m_low_out[...] = m_low
    near = product(faces_high[...], faces_low[...], m_high, m_low)
    near_x_out[...] = near[:FSLOT]
    near_y_out[...] = near[FSLOT:]


def last_kernel(count, everything, m, gradient, floor, out, out_here, sems):
    squares = jnp.sum(everything[...], axis=0)
    rate = step_length / jnp.sqrt(squares / count + epsilon)
    copies = []
    for number in range(CHUNKS):
        part = chunk(number)
        lowest = jnp.concatenate([floor[part, :].astype(f32)] * (COLS // FSLOT), axis=1)
        out_here[:, part] = jnp.maximum(m[part, :] - gradient[part, :] * rate, lowest).T
        where = pl.ds(number * COLS, COLS)
        copies.append(pltpu.make_async_copy(out_here.at[:, where], out.at[:, where], sems.at[number]))
        copies[-1].start()
    for copy in copies:
        copy.wait()


HERE = pl.BlockSpec(memory_space=pltpu.VMEM)
ANY = pl.BlockSpec(memory_space=pl.ANY)


def outside(x):
    return pltpu.with_memory_space_constraint(x, pltpu.HBM)


def far(x):
    return outside(x), ANY


def kept(x):
    return pltpu.with_memory_space_constraint(x, pltpu.VMEM), HERE


def keep(shape, dtype):
    return pltpu.VMEM(shape, dtype), HERE


def call(kernel, outs, args, scratch=()):
    return pl.pallas_call(
        kernel,
        out_shape=tuple(shape for shape, _ in outs),
        in_specs=[spec for _, spec in args],
        out_specs=tuple(spec for _, spec in outs),
        scratch_shapes=list(scratch),
        compiler_params=pltpu.CompilerParams(vmem_limit_bytes=24 * 2**20),
    )(*(arg for arg, _ in args))


def swapped(block, axis, first):
    route = []
    for i in range(first, lax.axis_size(axis) - 1, 2):
        route += [(i, i + 1), (i + 1, i)]
    return lax.ppermute(block, axis, route)


def swapped_by_core(block, first):
    route = []
    rows = lax.axis_size(GY)
    for core in range(lax.axis_size("c")):
        for i in range((first + core) % 2, rows - 1, 2):
            here = core * rows + i
            route += [(here, here + 1), (here + 1, here)]
    return lax.ppermute(block, NEAR, route)


def from_everyone(copies, axis):
    return lax.all_to_all(copies, axis, split_axis=0, concat_axis=0, tiled=True)


def body(operator, loads, warm, orders, face_x, face_y, contact):
    count = float(lax.axis_size(GX) * lax.axis_size(GY) * ORDER)
    orders = orders.T
    square = keep((ORDER, ORDER), bf16)
    faces = keep((2 * FSLOT, ORDER), bf16)
    state = keep((ORDER, COLS), f32)
    half = keep((ORDER, COLS), bf16)
    face = keep((FSLOT, COLS), f32)
    rows_here = pltpu.VMEM((ORDER, ORDER), f32)
    orders_here = pltpu.SMEM(orders.shape, jnp.int32)
    loads_here = pltpu.VMEM((COLS, ORDER), f32)
    sems = pltpu.SemaphoreType.DMA((CHUNKS,))
    high, low, faces_high, faces_low, slots, floor, rhs, m, m_high, m_low, near_x, near_y = call(
        first_kernel,
        [square, square, faces, faces, keep((2, FSLOT), jnp.int32), keep((ORDER, FSLOT), bf16), state, state, half, half, face, face],
        [far(x) for x in (orders, operator[0, 0], warm[0, 0], loads[0, 0], face_x[0], face_y[0], contact[0])],
        [orders_here, rows_here, loads_here, loads_here, pltpu.VMEM((1, ORDER), jnp.int32), sems, pltpu.SemaphoreType.DMA((6,))],
    )
    for iteration in range(ITERS):
        below = swapped_by_core(near_y, 0)
        above = swapped_by_core(near_y, 1)
        outer = swapped(near_x, GX, 1)
        inner = swapped(near_x, GX, 0)
        matrices = [kept(x) for x in (high, low, m_high, m_low)]
        (local,) = call(main_kernel, [state], [*matrices, kept(rhs)])
        gradient, squares = call(
            gradient_kernel, [state, keep((lax.axis_size(NEAR), 1, COLS), f32)],
            [kept(x) for x in (slots, local, outer, inner, below, above)],
        )
        (squares,) = call(
            middle_kernel, [keep((lax.axis_size(FAR), 1, COLS), f32)], [kept(from_everyone(squares, NEAR))]
        )
        everything = from_everyone(squares, FAR)
        given = [kept(x) for x in (everything, m, gradient, floor)]
        if iteration < ITERS - 1:
            m, m_high, m_low, near_x, near_y = call(
                functools.partial(update_kernel, count), [state, half, half, face, face],
                [*given, kept(faces_high), kept(faces_low)],
            )
        else:
            (out,) = call(
                functools.partial(last_kernel, count),
                [(pltpu.HBM((COLS, ORDER), f32), ANY)], given, [loads_here, sems],
            )
    return out[None, None]


def solution(mesh):
    shape = dict(mesh.shape)
    finer = Mesh(mesh.devices.reshape(shape["gx"] // 2, 2, 4, shape["gy"] // 4), ("z", "c", "y", "x"))
    in_specs = (
        P(GX, GY, None, None),
        P(GX, GY, None, None),
        P(GX, GY, None, None),
        P(),
        P(GX, GY, None),
        P(GX, GY, None),
        P(GX, GY, None),
    )
    out_specs = P(GX, GY, None, None)
    return jax.shard_map(body, mesh=finer, in_specs=in_specs, out_specs=out_specs, check_vma=False)
```

```python
import functools

import jax
import jax.numpy as jnp
from jax import lax
from jax.experimental import pallas as pl
from jax.experimental.pallas import tpu as pltpu
from jax.sharding import Mesh
from jax.sharding import PartitionSpec as P

ORDER = 768
FSLOT = 128
COLS = 256
ITERS = 3
CHUNKS = ORDER // COLS
GX = ("z1", "z0", "c")
GY = ("y", "x")
NEAR = ("c", "y", "x")
FAR = ("z0", "z1")

step_length = 0.5
epsilon = 1e-06

f32 = jnp.float32
bf16 = jnp.bfloat16


def dot(a, b):
    return lax.dot_general(a, b, (((1,), (0,)), ((), ())), preferred_element_type=f32)


def split(x):
    high = x.astype(bf16)
    return high, (x - high.astype(f32)).astype(bf16)


def product(a_high, a_low, m_high, m_low):
    return dot(a_high, m_high) + (dot(a_high, m_low) + dot(a_low, m_high))


def live_rows(order, columns):
    return lax.broadcasted_iota(jnp.int32, (ORDER, columns), 0) < order


def chunk(number):
    return slice(number * COLS, (number + 1) * COLS)


def chunk_copies(source, target, sems):
    return [
        pltpu.make_async_copy(source.at[:, pl.ds(number * COLS, COLS)], target.at[:, pl.ds(number * COLS, COLS)], sems.at[number])
        for number in range(CHUNKS)
    ]


def first_kernel(orders, operator, warm, loads, face_x, face_y, contact,
                 high_out, low_out, faces_high_out, faces_low_out, slots_out, floor_out, rhs_out, m_out, m_high_out, m_low_out, near_x_out, near_y_out,
                 orders_here, rows_here, warm_here, loads_here, contact_here, sems, small_sems):
    small = [
        pltpu.make_async_copy(face_x, slots_out.at[0:1, :], small_sems.at[0]),
        pltpu.make_async_copy(face_y, slots_out.at[1:2, :], small_sems.at[1]),
        pltpu.make_async_copy(orders, orders_here, small_sems.at[2]),
        pltpu.make_async_copy(warm, warm_here, small_sems.at[3]),
        pltpu.make_async_copy(contact, contact_here, small_sems.at[4]),
        pltpu.make_async_copy(loads, loads_here, small_sems.at[5]),
    ]
    for copy in small[:5]:
        copy.start()
    copies = chunk_copies(operator, rows_here, sems)
    for copy in copies:
        copy.start()
    small[5].start()
    small[0].wait()
    small[1].wait()
    column = jnp.concatenate([jnp.broadcast_to(slots_out[n : n + 1, :].astype(f32), (FSLOT, FSLOT)).T for n in range(2)], axis=0)
    wide = jnp.concatenate([column] * (ORDER // FSLOT), axis=1)
    lanes = lax.broadcasted_iota(jnp.int32, (2 * FSLOT, ORDER), 1).astype(f32)
    pick = jnp.where(wide == lanes, 1.0, 0.0).astype(bf16)
    small[4].wait()
    floor = jnp.where(contact_here[...] == 1, 0.0, -jnp.inf)
    floor_out[...] = jnp.broadcast_to(floor, (FSLOT, ORDER)).T.astype(bf16)
    small[2].wait()
    small[3].wait()
    order = order_of(orders_here)
    m = jnp.where(live_rows(order, COLS), warm_here[...].T, 0.0)
    m_out[...] = m
    m_high, m_low = split(m)
    m_high_out[...] = m_high
    m_low_out[...] = m_low
    near = jnp.zeros((2 * FSLOT, COLS), f32)
    for number, copy in enumerate(copies):
        copy.wait()
        if number == 1:
            small[5].wait()
            rhs_out[...] = jnp.where(live_rows(order, COLS), loads_here[...].T, 0.0)
        part = chunk(number)
        high, low = split(jnp.where(live_rows(order, COLS), rows_here[:, part], 0.0))
        high_out[:, part] = high
        low_out[:, part] = low
        face_high = dot(pick, high).astype(bf16)
        face_low = dot(pick, low).astype(bf16)
        faces_high_out[:, part] = face_high
        faces_low_out[:, part] = face_low
        near += product(face_high, face_low, m_high_out[part, :], m_low_out[part, :])
    near_x_out[...] = near[:FSLOT]
    near_y_out[...] = near[FSLOT:]


def order_of(orders):
    return orders[lax.axis_index(GY), lax.axis_index(GX)]


def main_kernel(high, low, m_high, m_low, rhs, local_out):
    local_out[...] = product(high[...], low[...], m_high[...], m_low[...]) - rhs[...]


def middle_kernel(everything, out):
    total = jnp.sum(everything[...], axis=0)
    out[...] = jnp.broadcast_to(total[None], out.shape)


def gradient_kernel(slots, local, outer, inner, below, above, gradient_out, squares_out):
    rows = lax.broadcasted_iota(jnp.int32, (ORDER, FSLOT), 0)
    spots = jnp.concatenate([jnp.where(rows == slots[number : number + 1, :], 1.0, 0.0).astype(bf16) for number in range(2)], axis=1)
    sums = jnp.concatenate([outer[...] + inner[...], below[...] + above[...]], axis=0)
    sum_high, sum_low = split(sums)
    gradient = local[...] - (dot(spots, sum_high) + dot(spots, sum_low))
    gradient_out[...] = gradient
    squares = jnp.sum(gradient * gradient, axis=0, keepdims=True)
    squares_out[...] = jnp.broadcast_to(squares[None], squares_out.shape)


def updated(everything, m, gradient, floor, count):
    squares = jnp.sum(everything[...], axis=0)
    rate = step_length / jnp.sqrt(squares / count + epsilon)
    lowest = jnp.concatenate([floor[...].astype(f32)] * (COLS // FSLOT), axis=1)
    return jnp.maximum(m[...] - gradient[...] * rate, lowest)


def update_kernel(count, everything, m, gradient, floor, faces_high, faces_low, m_out, m_high_out, m_low_out, near_x_out, near_y_out):
    new = updated(everything, m, gradient, floor, count)
    m_out[...] = new
    m_high, m_low = split(new)
    m_high_out[...] = m_high
    m_low_out[...] = m_low
    near = product(faces_high[...], faces_low[...], m_high, m_low)
    near_x_out[...] = near[:FSLOT]
    near_y_out[...] = near[FSLOT:]


def last_kernel(count, everything, m, gradient, floor, out, out_here, sems):
    squares = jnp.sum(everything[...], axis=0)
    rate = step_length / jnp.sqrt(squares / count + epsilon)
    copies = []
    for number in range(CHUNKS):
        part = chunk(number)
        lowest = jnp.concatenate([floor[part, :].astype(f32)] * (COLS // FSLOT), axis=1)
        out_here[:, part] = jnp.maximum(m[part, :] - gradient[part, :] * rate, lowest).T
        where = pl.ds(number * COLS, COLS)
        copies.append(pltpu.make_async_copy(out_here.at[:, where], out.at[:, where], sems.at[number]))
        copies[-1].start()
    for copy in copies:
        copy.wait()


HERE = pl.BlockSpec(memory_space=pltpu.VMEM)
ANY = pl.BlockSpec(memory_space=pl.ANY)


def outside(x):
    return pltpu.with_memory_space_constraint(x, pltpu.HBM)


def far(x):
    return outside(x), ANY


def kept(x):
    return pltpu.with_memory_space_constraint(x, pltpu.VMEM), HERE


def keep(shape, dtype):
    return pltpu.VMEM(shape, dtype), HERE


def call(kernel, outs, args, scratch=()):
    return pl.pallas_call(
        kernel,
        out_shape=tuple(shape for shape, _ in outs),
        in_specs=[spec for _, spec in args],
        out_specs=tuple(spec for _, spec in outs),
        scratch_shapes=list(scratch),
        compiler_params=pltpu.CompilerParams(vmem_limit_bytes=24 * 2**20),
    )(*(arg for arg, _ in args))


def swapped(block, axis, first):
    route = []
    for i in range(first, lax.axis_size(axis) - 1, 2):
        route += [(i, i + 1), (i + 1, i)]
    return lax.ppermute(block, axis, route)


def swapped_by_core(block, first):
    route = []
    rows = lax.axis_size(GY)
    for core in range(lax.axis_size("c")):
        for i in range((first + core) % 2, rows - 1, 2):
            here = core * rows + i
            route += [(here, here + 1), (here + 1, here)]
    return lax.ppermute(block, ("c", "y", "x"), route)


def from_everyone(copies, axis):
    return lax.all_to_all(copies, axis, split_axis=0, concat_axis=0, tiled=True)


def body(operator, loads, warm, orders, face_x, face_y, contact):
    count = float(lax.axis_size(GX) * lax.axis_size(GY) * ORDER)
    orders = orders.T
    square = keep((ORDER, ORDER), bf16)
    faces = keep((2 * FSLOT, ORDER), bf16)
    state = keep((ORDER, COLS), f32)
    half = keep((ORDER, COLS), bf16)
    face = keep((FSLOT, COLS), f32)
    rows_here = pltpu.VMEM((ORDER, ORDER), f32)
    orders_here = pltpu.SMEM(orders.shape, jnp.int32)
    loads_here = pltpu.VMEM((COLS, ORDER), f32)
    sems = pltpu.SemaphoreType.DMA((CHUNKS,))
    high, low, faces_high, faces_low, slots, floor, rhs, m, m_high, m_low, near_x, near_y = call(
        first_kernel,
        [square, square, faces, faces, keep((2, FSLOT), jnp.int32), keep((ORDER, FSLOT), bf16), state, state, half, half, face, face],
        [far(x) for x in (orders, operator[0, 0], warm[0, 0], loads[0, 0], face_x[0], face_y[0], contact[0])],
        [orders_here, rows_here, loads_here, loads_here, pltpu.VMEM((1, ORDER), jnp.int32), sems, pltpu.SemaphoreType.DMA((6,))],
    )
    for iteration in range(ITERS):
        below = swapped_by_core(near_y, 0)
        above = swapped_by_core(near_y, 1)
        outer = swapped(near_x, GX, 1)
        inner = swapped(near_x, GX, 0)
        matrices = [kept(x) for x in (high, low, m_high, m_low)]
        (local,) = call(main_kernel, [state], [*matrices, kept(rhs)])
        gradient, squares = call(
            gradient_kernel, [state, keep((lax.axis_size(NEAR), 1, COLS), f32)],
            [kept(x) for x in (slots, local, outer, inner, below, above)],
        )
        (squares,) = call(
            middle_kernel, [keep((lax.axis_size(FAR), 1, COLS), f32)], [kept(from_everyone(squares, NEAR))]
        )
        everything = from_everyone(squares, FAR)
        given = [kept(x) for x in (everything, m, gradient, floor)]
        if iteration < ITERS - 1:
            m, m_high, m_low, near_x, near_y = call(
                functools.partial(update_kernel, count), [state, half, half, face, face],
                [*given, kept(faces_high), kept(faces_low)],
            )
        else:
            (out,) = call(
                functools.partial(last_kernel, count),
                [(pltpu.HBM((COLS, ORDER), f32), ANY)], given, [loads_here, sems],
            )
    return out[None, None]


def solution(mesh):
    shape = dict(mesh.shape)
    finer = Mesh(mesh.devices.reshape(4, shape["gx"] // 8, 2, 4, shape["gy"] // 4), ("z1", "z0", "c", "y", "x"))
    in_specs = (
        P(GX, GY, None, None),
        P(GX, GY, None, None),
        P(GX, GY, None, None),
        P(),
        P(GX, GY, None),
        P(GX, GY, None),
        P(GX, GY, None),
    )
    out_specs = P(GX, GY, None, None)
    return jax.shard_map(body, mesh=finer, in_specs=in_specs, out_specs=out_specs, check_vma=False)
```

```python
import functools

import jax
import jax.numpy as jnp
from jax import lax
from jax.experimental import pallas as pl
from jax.experimental.pallas import tpu as pltpu
from jax.sharding import Mesh
from jax.sharding import PartitionSpec as P

ORDER = 768
FSLOT = 128
COLS = 256
ITERS = 3
CHUNKS = ORDER // COLS
GX = ("z1", "z0", "c")
GY = ("y", "x")
NEAR = ("c", "y", "x")
FAR = ("z0", "z1")

step_length = 0.5
epsilon = 1e-06

f32 = jnp.float32
bf16 = jnp.bfloat16


def dot(a, b):
    return lax.dot_general(a, b, (((1,), (0,)), ((), ())), preferred_element_type=f32)


def split(x):
    high = x.astype(bf16)
    return high, (x - high.astype(f32)).astype(bf16)


def product(a_high, a_low, m_high, m_low):
    return dot(a_high, m_high) + (dot(a_high, m_low) + dot(a_low, m_high))


def live_rows(order, columns):
    return lax.broadcasted_iota(jnp.int32, (ORDER, columns), 0) < order


def chunk(number):
    return slice(number * COLS, (number + 1) * COLS)


def chunk_copies(source, target, sems):
    return [
        pltpu.make_async_copy(source.at[:, pl.ds(number * COLS, COLS)], target.at[:, pl.ds(number * COLS, COLS)], sems.at[number])
        for number in range(CHUNKS)
    ]


def first_kernel(orders, operator, warm, loads, face_x, face_y, contact,
                 high_out, low_out, faces_high_out, faces_low_out, slots_out, floor_out, rhs_out, m_out, m_high_out, m_low_out, near_x_out, near_y_out,
                 orders_here, rows_here, warm_here, loads_here, contact_here, sems, small_sems):
    small = [
        pltpu.make_async_copy(face_x, slots_out.at[0:1, :], small_sems.at[0]),
        pltpu.make_async_copy(face_y, slots_out.at[1:2, :], small_sems.at[1]),
        pltpu.make_async_copy(orders, orders_here, small_sems.at[2]),
        pltpu.make_async_copy(warm, warm_here, small_sems.at[3]),
        pltpu.make_async_copy(contact, contact_here, small_sems.at[4]),
        pltpu.make_async_copy(loads, loads_here, small_sems.at[5]),
    ]
    for copy in small[:5]:
        copy.start()
    copies = chunk_copies(operator, rows_here, sems)
    for copy in copies:
        copy.start()
    small[5].start()
    small[0].wait()
    small[1].wait()
    column = jnp.concatenate([jnp.broadcast_to(slots_out[n : n + 1, :].astype(f32), (FSLOT, FSLOT)).T for n in range(2)], axis=0)
    wide = jnp.concatenate([column] * (ORDER // FSLOT), axis=1)
    lanes = lax.broadcasted_iota(jnp.int32, (2 * FSLOT, ORDER), 1).astype(f32)
    pick = jnp.where(wide == lanes, 1.0, 0.0).astype(bf16)
    small[4].wait()
    floor = jnp.where(contact_here[...] == 1, 0.0, -jnp.inf)
    floor_out[...] = jnp.broadcast_to(floor, (FSLOT, ORDER)).T.astype(bf16)
    small[2].wait()
    small[3].wait()
    order = order_of(orders_here)
    m = jnp.where(live_rows(order, COLS), warm_here[...].T, 0.0)
    m_out[...] = m
    m_high, m_low = split(m)
    m_high_out[...] = m_high
    m_low_out[...] = m_low
    near = jnp.zeros((2 * FSLOT, COLS), f32)
    for number, copy in enumerate(copies):
        copy.wait()
        if number == 1:
            small[5].wait()
            rhs_out[...] = jnp.where(live_rows(order, COLS), loads_here[...].T, 0.0)
        part = chunk(number)
        high, low = split(jnp.where(live_rows(order, COLS), rows_here[:, part], 0.0))
        high_out[:, part] = high
        low_out[:, part] = low
        face_high = dot(pick, high).astype(bf16)
        face_low = dot(pick, low).astype(bf16)
        faces_high_out[:, part] = face_high
        faces_low_out[:, part] = face_low
        near += product(face_high, face_low, m_high_out[part, :], m_low_out[part, :])
    near_x_out[...] = near[:FSLOT]
    near_y_out[...] = near[FSLOT:]


def order_of(orders):
    return orders[lax.axis_index(GY), lax.axis_index(GX)]


def main_kernel(high, low, m_high, m_low, rhs, local_out):
    local_out[...] = product(high[...], low[...], m_high[...], m_low[...]) - rhs[...]


def middle_kernel(everything, out):
    total = jnp.sum(everything[...], axis=0)
    out[...] = jnp.broadcast_to(total[None], out.shape)


def gradient_kernel(slots, local, outer, inner, below, above, gradient_out, squares_out):
    rows = lax.broadcasted_iota(jnp.int32, (ORDER, FSLOT), 0)
    spots = jnp.concatenate([jnp.where(rows == slots[number : number + 1, :], 1.0, 0.0).astype(bf16) for number in range(2)], axis=1)
    sums = jnp.concatenate([outer[...] + inner[...], below[...] + above[...]], axis=0)
    sum_high, sum_low = split(sums)
    gradient = local[...] - (dot(spots, sum_high) + dot(spots, sum_low))
    gradient_out[...] = gradient
    squares = jnp.sum(gradient * gradient, axis=0, keepdims=True)
    squares_out[...] = jnp.broadcast_to(squares[None], squares_out.shape)


def update_kernel(count, everything, m, gradient, floor, faces_high, faces_low, m_out, m_high_out, m_low_out, near_x_out, near_y_out):
    squares = jnp.sum(everything[...], axis=0)
    rate = step_length / jnp.sqrt(squares / count + epsilon)
    near = jnp.zeros((2 * FSLOT, COLS), f32)
    for number in range(CHUNKS):
        part = chunk(number)
        lowest = jnp.concatenate([floor[part, :].astype(f32)] * (COLS // FSLOT), axis=1)
        new = jnp.maximum(m[part, :] - gradient[part, :] * rate, lowest)
        m_out[part, :] = new
        m_high, m_low = split(new)
        m_high_out[part, :] = m_high
        m_low_out[part, :] = m_low
        near += product(faces_high[:, part], faces_low[:, part], m_high, m_low)
    near_x_out[...] = near[:FSLOT]
    near_y_out[...] = near[FSLOT:]


def last_kernel(count, everything, m, gradient, floor, out, out_here, sems):
    squares = jnp.sum(everything[...], axis=0)
    rate = step_length / jnp.sqrt(squares / count + epsilon)
    copies = []
    for number in range(CHUNKS):
        part = chunk(number)
        lowest = jnp.concatenate([floor[part, :].astype(f32)] * (COLS // FSLOT), axis=1)
        out_here[:, part] = jnp.maximum(m[part, :] - gradient[part, :] * rate, lowest).T
        where = pl.ds(number * COLS, COLS)
        copies.append(pltpu.make_async_copy(out_here.at[:, where], out.at[:, where], sems.at[number]))
        copies[-1].start()
    for copy in copies:
        copy.wait()


HERE = pl.BlockSpec(memory_space=pltpu.VMEM)
ANY = pl.BlockSpec(memory_space=pl.ANY)


def outside(x):
    return pltpu.with_memory_space_constraint(x, pltpu.HBM)


def far(x):
    return outside(x), ANY


def kept(x):
    return pltpu.with_memory_space_constraint(x, pltpu.VMEM), HERE


def keep(shape, dtype):
    return pltpu.VMEM(shape, dtype), HERE


def call(kernel, outs, args, scratch=()):
    return pl.pallas_call(
        kernel,
        out_shape=tuple(shape for shape, _ in outs),
        in_specs=[spec for _, spec in args],
        out_specs=tuple(spec for _, spec in outs),
        scratch_shapes=list(scratch),
        compiler_params=pltpu.CompilerParams(vmem_limit_bytes=24 * 2**20),
    )(*(arg for arg, _ in args))


def swapped(block, axis, first):
    route = []
    for i in range(first, lax.axis_size(axis) - 1, 2):
        route += [(i, i + 1), (i + 1, i)]
    return lax.ppermute(block, axis, route)


def swapped_by_core(block, first):
    route = []
    rows = lax.axis_size(GY)
    for core in range(lax.axis_size("c")):
        for i in range((first + core) % 2, rows - 1, 2):
            here = core * rows + i
            route += [(here, here + 1), (here + 1, here)]
    return lax.ppermute(block, ("c", "y", "x"), route)


def from_everyone(copies, axis):
    return lax.all_to_all(copies, axis, split_axis=0, concat_axis=0, tiled=True)


def body(operator, loads, warm, orders, face_x, face_y, contact):
    count = float(lax.axis_size(GX) * lax.axis_size(GY) * ORDER)
    orders = orders.T
    square = keep((ORDER, ORDER), bf16)
    faces = keep((2 * FSLOT, ORDER), bf16)
    state = keep((ORDER, COLS), f32)
    half = keep((ORDER, COLS), bf16)
    face = keep((FSLOT, COLS), f32)
    rows_here = pltpu.VMEM((ORDER, ORDER), f32)
    orders_here = pltpu.SMEM(orders.shape, jnp.int32)
    loads_here = pltpu.VMEM((COLS, ORDER), f32)
    sems = pltpu.SemaphoreType.DMA((CHUNKS,))
    high, low, faces_high, faces_low, slots, floor, rhs, m, m_high, m_low, near_x, near_y = call(
        first_kernel,
        [square, square, faces, faces, keep((2, FSLOT), jnp.int32), keep((ORDER, FSLOT), bf16), state, state, half, half, face, face],
        [far(x) for x in (orders, operator[0, 0], warm[0, 0], loads[0, 0], face_x[0], face_y[0], contact[0])],
        [orders_here, rows_here, loads_here, loads_here, pltpu.VMEM((1, ORDER), jnp.int32), sems, pltpu.SemaphoreType.DMA((6,))],
    )
    for iteration in range(ITERS):
        below = swapped_by_core(near_y, 0)
        above = swapped_by_core(near_y, 1)
        outer = swapped(near_x, GX, 1)
        inner = swapped(near_x, GX, 0)
        matrices = [kept(x) for x in (high, low, m_high, m_low)]
        (local,) = call(main_kernel, [state], [*matrices, kept(rhs)])
        gradient, squares = call(
            gradient_kernel, [state, keep((lax.axis_size(NEAR), 1, COLS), f32)],
            [kept(x) for x in (slots, local, outer, inner, below, above)],
        )
        (squares,) = call(
            middle_kernel, [keep((lax.axis_size(FAR), 1, COLS), f32)], [kept(from_everyone(squares, NEAR))]
        )
        everything = from_everyone(squares, FAR)
        given = [kept(x) for x in (everything, m, gradient, floor)]
        if iteration < ITERS - 1:
            m, m_high, m_low, near_x, near_y = call(
                functools.partial(update_kernel, count), [state, half, half, face, face],
                [*given, kept(faces_high), kept(faces_low)],
            )
        else:
            (out,) = call(
                functools.partial(last_kernel, count),
                [(pltpu.HBM((COLS, ORDER), f32), ANY)], given, [loads_here, sems],
            )
    return out[None, None]


def solution(mesh):
    shape = dict(mesh.shape)
    finer = Mesh(mesh.devices.reshape(4, shape["gx"] // 8, 2, 4, shape["gy"] // 4), ("z1", "z0", "c", "y", "x"))
    in_specs = (
        P(GX, GY, None, None),
        P(GX, GY, None, None),
        P(GX, GY, None, None),
        P(),
        P(GX, GY, None),
        P(GX, GY, None),
        P(GX, GY, None),
    )
    out_specs = P(GX, GY, None, None)
    return jax.shard_map(body, mesh=finer, in_specs=in_specs, out_specs=out_specs, check_vma=False)
```
